1024 devices in a mesh: dp: 16 (over z_hi, x, core), expert: 64 (over z_lo, y).
Axes of the slice: x: 4, y: 8, z: 16 (z_hi: 2, z_lo: 8; z = z_hi * 8 + z_lo), core: 2. Of those that a mesh axis runs over, the one named last changes fastest.
Arguments:
- tokens: bfloat16 [131072, 2048], P(('dp', 'expert')), may hold values from -6 to 6
- expert_ids: int32 [131072, 2], P(('dp', 'expert')), may hold values from 0 to 63, as said below
- gate_values: float32 [131072, 2], P(('dp', 'expert')), may hold values from 0.25 to 1
- capacity: int32 [32], replicated, may hold values from 2 to 4, as said below
- w_in: bfloat16 [64, 2048, 1024], P('expert', 'dp'), may hold values from -0.125 to 0.125
- w_down: bfloat16 [64, 512, 2048], P('expert', None, 'dp'), may hold values from -0.1875 to 0.1875
Outputs:
- mixed: bfloat16 [131072, 2048], P(('dp', 'expert'))
The draws below stay inside these ranges and needn't reach their ends.
Inputs may be any that keep to these rules, and one draw needn't show every extreme that they name: `expert_ids`: A token's two ids differ. One expert, the busy one, has capacity 4 and is named by the first 4 tokens of every source. The busy expert's capacity is 4.
All inputs are finite; a program needn't handle non-finite values.
Results may differ from the reference program's by a relative error of at most 0.0065.
Values may be sent and summed in bfloat16 or wider, within the bound.
A program may use at most 32 MiB of HBM per device.

```python
import jax
import jax.numpy as jnp
from jax import lax

D = 2048
HH = 512
CAP = 4
TOK_DEV = 128
TOKENS = 131072
EXPERTS_ALL = 64
EXPERTS = 32
N_DP = 16
N_EXPERT = 64


def pick_busy(key):
    return jax.random.randint(jax.random.fold_in(key, 11), (), 0, EXPERTS)


def draw_capacity(key, part):
    base_values = jax.random.randint(jax.random.fold_in(key, 3), (EXPERTS,), 2, CAP + 1)
    return base_values.at[pick_busy(key)].set(CAP).astype(jnp.int32)


def draw_expert_ids(key, part):
    keys = jax.random.split(jax.random.fold_in(key, 5), 5)
    pick_one = jax.random.randint(keys[0], (TOKENS,), 0, EXPERTS_ALL)
    pick_two = jax.random.randint(keys[1], (TOKENS,), 0, EXPERTS_ALL)
    pick_three = jax.random.randint(keys[2], (TOKENS,), 0, EXPERTS_ALL)
    lowest = jnp.minimum(jnp.minimum(pick_one, pick_two), pick_three)
    shuffled = jax.random.permutation(keys[3], EXPERTS_ALL)
    first_pick = shuffled[lowest]
    offsets = jax.random.randint(keys[4], (TOKENS,), 1, EXPERTS_ALL)
    second_pick = (first_pick + offsets) % EXPERTS_ALL
    busy = pick_busy(key)
    position = jnp.arange(TOKENS) % TOK_DEV
    forced = position < CAP
    first_pick = jnp.where(forced, busy, first_pick)
    second_pick = jnp.where(forced & (second_pick == busy), (busy + 1) % EXPERTS_ALL, second_pick)
    return jnp.stack([first_pick, second_pick], axis=1).astype(jnp.int32)


def block_levels(key, dims, cuts, low, largest):
    gain = 1.0
    for dim, blocks in cuts:
        steps = jax.random.uniform(jax.random.fold_in(jax.random.fold_in(key, 6), dim), (blocks,), jnp.float32, low / len(cuts), largest / len(cuts))
        gain = gain * jnp.repeat(jnp.exp(steps), dims[dim] // blocks).reshape((-1,) + (1,) * (len(dims) - 1 - dim))
    return gain


def noise(key, extent, deviation, reach, cuts=(), kind=jnp.bfloat16):
    values = deviation * jax.random.normal(key, extent, jnp.float32)
    if cuts:
        values = values * block_levels(key, extent, cuts, -0.22, 0.18)
    return jnp.clip(values, -reach, reach).astype(kind)


def setup_inputs(seed: int = 0) -> dict:
    streams_of = jax.random.split(jax.random.key(seed), 7)
    return {
        "tokens": noise(streams_of[0], (TOKENS, D), 1.0, 6.0, ((0, 1024),)),
        "expert_ids": draw_expert_ids(jax.random.fold_in(streams_of[6], 71), 0),
        "gate_values": jnp.clip(0.25 + 0.75 * jax.random.uniform(streams_of[2], (TOKENS, 2), jnp.float32) ** block_levels(streams_of[2], (TOKENS, 2), ((0, 1024),), -0.2, 0.2), 0.25, 1.0),
        "capacity": draw_capacity(jax.random.fold_in(streams_of[6], 71), 0),
        "w_in": noise(streams_of[4], (2 * EXPERTS, D, 2 * HH), D ** -0.5, 0.125, ((0, 64), (1, 16))),
        "w_down": noise(streams_of[5], (2 * EXPERTS, HH, D), (2 * HH) ** -0.5, 0.1875, ((0, 64), (2, 16))),
    }


def expert_half(token_rows, weight_in, weight_down):
    gate_up = jnp.dot(token_rows, weight_in, preferred_element_type=jnp.float32)
    hidden = (jax.nn.silu(gate_up[:, :HH]) * gate_up[:, HH:]).astype(jnp.bfloat16)
    return jnp.dot(hidden, weight_down, preferred_element_type=jnp.float32).astype(jnp.bfloat16)


def reference(tokens, expert_ids, gate_values, capacity, w_in, w_down):
    sources = TOKENS // TOK_DEV
    assigned = TOK_DEV * 2
    flat_ids = expert_ids.reshape(sources, assigned)
    expert_range = jnp.arange(EXPERTS, dtype=jnp.int32)
    one_hot = (flat_ids[:, :, None] == expert_range[None, None, :]).astype(jnp.int32)
    slot_rank = jnp.sum((jnp.cumsum(one_hot, axis=1) - one_hot) * one_hot, axis=2)
    slot_limit = jnp.sum(one_hot * capacity[None, None, :], axis=2)
    kept_mask = (jnp.sum(one_hot, axis=2) > 0) & (slot_rank < slot_limit)
    slot_index = jnp.where(kept_mask, flat_ids * CAP + slot_rank, EXPERTS * CAP).astype(jnp.int32)
    source_rows = jnp.broadcast_to(jnp.arange(sources, dtype=jnp.int32)[:, None], (sources, assigned))
    assign_range = jnp.broadcast_to(jnp.arange(assigned, dtype=jnp.int32)[None, :], (sources, assigned))
    table = jnp.full((sources, EXPERTS * CAP + 1), -1, dtype=jnp.int32)
    table = table.at[source_rows, slot_index].set(assign_range)[:, :EXPERTS * CAP]
    filled = table >= 0
    safe_index = jnp.maximum(table, 0).astype(jnp.int32)
    flat_gates = gate_values.reshape(sources, assigned)
    slot_weight = jnp.where(filled, jnp.take_along_axis(flat_gates, safe_index, axis=1), jnp.float32(0.0))
    local_source = (jnp.arange(sources, dtype=jnp.int32) % N_EXPERT)[:, None]
    token_index = (local_source * TOK_DEV + safe_index // 2).astype(jnp.int32)
    group_tokens = N_EXPERT * TOK_DEV

    def regroup(values):
        shaped = values.reshape(N_DP, N_EXPERT, EXPERTS, CAP)
        return jnp.transpose(shaped, (0, 2, 1, 3)).reshape(N_DP, EXPERTS, N_EXPERT * CAP)

    index_groups = regroup(token_index)
    weight_groups = regroup(slot_weight)
    filled_groups = regroup(filled)
    token_groups = tokens.reshape(N_DP, group_tokens, D)
    paired_in = w_in.reshape(EXPERTS, 2, D, 2 * HH)
    paired_down = w_down.reshape(EXPERTS, 2, HH, D)

    def one_group(group_args):
        group_rows, group_index, group_weight, group_filled = group_args

        def one_expert(running, expert_args):
            slot_tokens, slot_gates, slot_filled, pair_in, pair_down = expert_args
            token_rows = jnp.where(slot_filled[:, None], group_rows[slot_tokens], 0)
            first_part = expert_half(token_rows, pair_in[0], pair_down[0])
            second_part = expert_half(token_rows, pair_in[1], pair_down[1])
            combined = (first_part.astype(jnp.float32) + second_part.astype(jnp.float32)).astype(jnp.bfloat16)
            combined = lax.optimization_barrier(combined).astype(jnp.float32)
            running = running.at[slot_tokens].add(slot_gates[:, None] * combined)
            return running, None

        start = jnp.zeros((group_tokens, D), dtype=jnp.float32)
        running, unused = lax.scan(one_expert, start, (group_index, group_weight, group_filled, paired_in, paired_down))
        return running

    mixed = lax.map(one_group, (token_groups, index_groups, weight_groups, filled_groups))
    return mixed.reshape(TOKENS, D).astype(jnp.bfloat16)
```

```python
import jax
import jax.numpy as jnp
from jax import lax
from jax.experimental import pallas as pl
from jax.experimental.pallas import tpu as pltpu
from jax.sharding import PartitionSpec as P

NX = 4
NC = 2
ZL = 8
NY = 8
NK = NY // 2
ZBLK = 16
YBLK = 32
MESH = pl.DeviceIdType.MESH
BF = jnp.bfloat16
F32 = jnp.float32


def mo(value, multiple):
    return pl.multiple_of(value, multiple)


def layer_kernel(
    tok_hbm, ids_ref, gate_ref, cap_ref, win_hbm, wdn_hbm, out_ref,
    tok, slots_out, slots_z, slots_y, rows, w_in, w_down, relay_in, relay_down,
    acc, hidden, partial, from_y, to_z, from_z, mix,
    load_sem, z1_send, z1_recv, y1_send, y1_recv, w_send, w_recv, relay_recv,
    y2_send, y2_recv, z2_send, z2_recv,
):
    dp = lax.axis_index("dp")
    ex = lax.axis_index("expert")
    zh = dp // (NX * NC)
    xi = (dp // NC) % NX
    core = dp % NC
    zl = ex // NY
    yi = ex % NY

    def dp_of(h, x, c):
        return h * (NX * NC) + x * NC + c

    sibling = (dp_of(zh, xi, 1 - core), ex)
    x_up = (xi + 1) % NX
    x_down = (xi + NX - 1) % NX
    dev_up = (dp_of(zh, x_up, core), ex)
    dev_down = (dp_of(zh, x_down, core), ex)
    sign = 1 - 2 * core
    z_all = zh * ZL + zl
    z_next = (z_all + (ZL // 2) * sign + 2 * ZL) % (2 * ZL)
    dev_relay = (dp_of(z_next // ZL, xi, core), (z_next % ZL) * NY + yi)
    z_prev = (z_all - (ZL // 2) * sign + 2 * ZL) % (2 * ZL)
    relay_slot = dp_of(z_prev // ZL, xi, core)
    dev_cross = (dp_of(1 - zh, xi, core), ((zl + ZL // 2) % ZL) * NY + yi)

    def dev_z(z):
        return (dp, z * NY + yi)

    def dev_y(y):
        return (dp, zl * NY + y)

    barrier = pltpu.get_barrier_semaphore()
    for peer in (sibling, dev_up, dev_down, dev_cross):
        pl.semaphore_signal(barrier, inc=1, device_id=peer, device_id_type=MESH)

    def greet(d, carry):
        pl.semaphore_signal(barrier, inc=1, device_id=dev_y((yi + d) % NY), device_id_type=MESH)
        pl.semaphore_signal(barrier, inc=1, device_id=dev_z((zl + d) % ZL), device_id_type=MESH)
        return carry

    lax.fori_loop(1, ZL, greet, 0)

    load_tok = pltpu.make_async_copy(tok_hbm, tok, load_sem.at[0])
    load_in = pltpu.make_async_copy(
        win_hbm, w_in.at[pl.ds(mo(dp * 128, 128), 128), :], load_sem.at[1]
    )
    load_down = pltpu.make_async_copy(wdn_hbm, w_down.at[dp], load_sem.at[2])
    load_in.start()
    load_tok.start()
    load_down.start()

    row = lax.broadcasted_iota(jnp.int32, (128, 128), 0)
    col = lax.broadcasted_iota(jnp.int32, (128, 128), 1)
    expert = row >> 2
    slot = row & 3
    first = ids_ref[0:1, :] == expert
    second = ids_ref[1:2, :] == expert
    named = jnp.where(first, 1.0, 0.0) + jnp.where(second, 1.0, 0.0)
    before = jnp.where(row < col, 1.0, 0.0).astype(BF)
    rank = jnp.dot(named.astype(BF), before, preferred_element_type=F32)
    wide_row = lax.broadcasted_iota(jnp.int32, (128, 32), 0)
    wide_col = lax.broadcasted_iota(jnp.int32, (128, 32), 1)
    cap_col = jnp.sum(
        jnp.where((wide_row >> 2) == wide_col, cap_ref[0:1, :].astype(F32), 0.0),
        axis=1,
        keepdims=True,
    )
    slot_f = slot.astype(F32)
    kept = (rank == slot_f) & (slot_f < cap_col)
    take_first = kept & first
    take_second = kept & second
    select = (jnp.where(take_first, 1.0, 0.0) + jnp.where(take_second, 1.0, 0.0)).astype(BF)
    weight = jnp.where(take_first, gate_ref[0:1, :], 0.0) + jnp.where(
        take_second, gate_ref[1:2, :], 0.0
    )
    weight = weight.T
    for part in range(3):
        piece_w = weight.astype(BF)
        mix[part] = piece_w
        weight = weight - piece_w.astype(F32)
    load_tok.wait()
    slots_out[...] = jnp.dot(select, tok[...], preferred_element_type=F32).astype(BF)
    to_pairs = ((((row >> 2) & 7) * 16 + (row >> 5) * 4 + (row & 3)) == col)
    to_pairs = jnp.where(to_pairs, 1.0, 0.0).astype(BF)
    to_lines = ((((row >> 2) & 3) * 32 + (row >> 4) * 4 + (row & 3)) == col)
    to_lines = jnp.where(to_lines, 1.0, 0.0).astype(BF)

    load_in.wait()
    load_down.wait()
    pl.semaphore_wait(barrier, 4 + 2 * (ZL - 1))

    sends = []

    def piece(p, i):
        if p == 2:
            return w_down.at[i]
        return w_in.at[pl.ds(mo(i * 128 + 64 * p, 64), 64), :]

    def relay_piece(p):
        if p == 2:
            return relay_down
        return relay_in.at[pl.ds(64 * p, 64), :]

    counter = [0, 0, 0]

    def send_to(p, src, dst, recv, dev):
        k = counter[p]
        counter[p] += 1
        copy = pltpu.make_async_remote_copy(
            src_ref=src, dst_ref=dst, send_sem=w_send.at[p, k], recv_sem=recv,
            device_id=dev, device_id_type=MESH,
        )
        copy.start()
        sends.append(copy)

    def send_piece(p, i, dev):
        send_to(p, piece(p, i), piece(p, i), w_recv.at[p, i], dev)

    def wait_piece(p, i):
        pltpu.make_async_remote_copy(
            src_ref=piece(p, i), dst_ref=piece(p, i), send_sem=w_send.at[p, 0],
            recv_sem=w_recv.at[p, i], device_id=sibling, device_id_type=MESH,
        ).wait_recv()

    def send_own(p, h):
        i = dp_of(h, xi, core)
        send_piece(p, i, dev_up)
        send_piece(p, i, dev_down)
        send_piece(p, i, sibling)

    def send_relay(p):
        send_to(p, piece(p, dp), relay_piece(p), relay_recv.at[p], dev_relay)

    def pass_relay(p):
        pltpu.make_async_remote_copy(
            src_ref=relay_piece(p), dst_ref=relay_piece(p), send_sem=w_send.at[p, 0],
            recv_sem=relay_recv.at[p], device_id=sibling, device_id_type=MESH,
        ).wait_recv()
        send_to(p, relay_piece(p), piece(p, relay_slot), w_recv.at[p, relay_slot], dev_relay)

    def pass_near(p, h):
        step = 1 - 2 * ((core + p) % 2)
        src_x = (xi - step + NX) % NX
        dst_x = (xi + step + NX) % NX
        i = dp_of(h, src_x, core)
        wait_piece(p, i)
        send_piece(p, i, (dp_of(zh, dst_x, core), ex))
        send_piece(p, i, sibling)
        i = dp_of(h, dst_x, core)
        wait_piece(p, i)
        send_piece(p, i, sibling)

    def pass_far(p, h):
        i = dp_of(h, (xi + 2) % NX, core)
        wait_piece(p, i)
        send_piece(p, i, sibling)

    def wait_sibling(p, h):
        for j in range(NX):
            wait_piece(p, dp_of(h, (xi + j) % NX, 1 - core))

    def block_cols(h):
        return pl.ds(mo(((zh + h) % 2) * 1024, 1024), 1024)

    def z1_copy(h, d):
        z = (zl + d) % ZL
        return pltpu.make_async_remote_copy(
            src_ref=slots_out.at[pl.ds(mo(z * ZBLK, ZBLK), ZBLK), block_cols(h)],
            dst_ref=slots_z.at[pl.ds(mo(zl * ZBLK, ZBLK), ZBLK), block_cols(h)],
            send_sem=z1_send.at[h, d], recv_sem=z1_recv.at[h, zl],
            device_id=dev_z(z), device_id_type=MESH,
        )

    def z1_wait(h, d):
        z = (zl + d) % ZL
        pltpu.make_async_remote_copy(
            src_ref=slots_out.at[pl.ds(mo(z * ZBLK, ZBLK), ZBLK), block_cols(h)],
            dst_ref=slots_z.at[pl.ds(mo(z * ZBLK, ZBLK), ZBLK), block_cols(h)],
            send_sem=z1_send.at[h, d], recv_sem=z1_recv.at[h, z],
            device_id=dev_z(z), device_id_type=MESH,
        ).wait_recv()

    def y1_copy(h, d):
        y = (yi + d) % NY
        return pltpu.make_async_remote_copy(
            src_ref=slots_y.at[pl.ds(mo((y // 2) * YBLK, YBLK), YBLK), block_cols(h)],
            dst_ref=rows.at[pl.ds(mo(yi * YBLK, YBLK), YBLK), block_cols(h)],
            send_sem=y1_send.at[h, d], recv_sem=y1_recv.at[h, yi],
            device_id=dev_y(y), device_id_type=MESH,
        )

    def y1_wait(h, d):
        y = (yi + d) % NY
        pltpu.make_async_remote_copy(
            src_ref=slots_y.at[pl.ds(mo((y // 2) * YBLK, YBLK), YBLK), block_cols(h)],
            dst_ref=rows.at[pl.ds(mo(y * YBLK, YBLK), YBLK), block_cols(h)],
            send_sem=y1_send.at[h, d], recv_sem=y1_recv.at[h, y],
            device_id=dev_y(y), device_id_type=MESH,
        ).wait_recv()

    def chunk_slot(j):
        return ((zh + j // 2) % 2) * 8 + ((xi // 2 + j) % 2) * 4

    def chunk_cols(j):
        return pl.ds(mo(chunk_slot(j) * 128, 512), 512)

    def y2_copy(j, d):
        y = (yi + d) % NY
        return pltpu.make_async_remote_copy(
            src_ref=partial.at[pl.ds(mo(y * YBLK, YBLK), YBLK), chunk_cols(j)],
            dst_ref=from_y.at[pl.ds(mo(yi * YBLK, YBLK), YBLK), chunk_cols(j)],
            send_sem=y2_send.at[j, d], recv_sem=y2_recv.at[j, yi],
            device_id=dev_y(y), device_id_type=MESH,
        )

    def y2_wait(j, d):
        y = (yi + d) % NY
        pltpu.make_async_remote_copy(
            src_ref=partial.at[pl.ds(mo(y * YBLK, YBLK), YBLK), chunk_cols(j)],
            dst_ref=from_y.at[pl.ds(mo(y * YBLK, YBLK), YBLK), chunk_cols(j)],
            send_sem=y2_send.at[j, d], recv_sem=y2_recv.at[j, y],
            device_id=dev_y(y), device_id_type=MESH,
        ).wait_recv()

    def z2_copy(j, d):
        z = (zl + d) % ZL
        return pltpu.make_async_remote_copy(
            src_ref=to_z.at[pl.ds(mo(z * ZBLK, ZBLK), ZBLK), chunk_cols(j)],
            dst_ref=from_z.at[pl.ds(mo(zl * ZBLK, ZBLK), ZBLK), chunk_cols(j)],
            send_sem=z2_send.at[j, d], recv_sem=z2_recv.at[j, zl],
            device_id=dev_z(z), device_id_type=MESH,
        )

    def z2_wait(j, d):
        z = (zl + d) % ZL
        pltpu.make_async_remote_copy(
            src_ref=to_z.at[pl.ds(mo(z * ZBLK, ZBLK), ZBLK), chunk_cols(j)],
            dst_ref=from_z.at[pl.ds(mo(z * ZBLK, ZBLK), ZBLK), chunk_cols(j)],
            send_sem=z2_send.at[j, d], recv_sem=z2_recv.at[j, z],
            device_id=dev_z(z), device_id_type=MESH,
        ).wait_recv()

    def start_all(make, h):
        def body(d, carry):
            make(h, d).start()
            return carry

        lax.fori_loop(1, ZL, body, 0)

    def sent_all(make, h):
        def body(d, carry):
            make(h, d).wait_send()
            return carry

        lax.fori_loop(1, ZL, body, 0)

    def wait_all(wait, h):
        def body(d, carry):
            wait(h, d)
            return carry

        lax.fori_loop(1, ZL, body, 0)

    own_z = pl.ds(mo(zl * ZBLK, ZBLK), ZBLK)
    own_y = pl.ds(mo(yi * YBLK, YBLK), YBLK)
    own_pair = pl.ds(mo((yi // 2) * YBLK, YBLK), YBLK)

    for p in (0, 1):
        send_relay(p)
        send_own(p, zh)
    for h in (0, 1):
        start_all(z1_copy, h)
        slots_z[own_z, block_cols(h)] = slots_out[own_z, block_cols(h)]
    send_relay(2)
    send_own(2, zh)

    def spread(h):
        wait_all(z1_wait, h)
        slots_y[:, block_cols(h)] = jnp.dot(
            to_pairs, slots_z[:, block_cols(h)], preferred_element_type=F32
        ).astype(BF)
        start_all(y1_copy, h)
        rows[own_y, block_cols(h)] = slots_y[own_pair, block_cols(h)]

    zo = 1 - zh
    pass_near(0, zh)
    pass_near(1, zh)
    pass_relay(0)
    pass_relay(1)
    spread(0)
    pass_far(0, zh)
    pass_far(1, zh)
    pass_near(2, zh)
    spread(1)
    pass_relay(2)
    pass_far(2, zh)
    for p in (0, 1):
        i = dp_of(zo, xi, core)
        wait_piece(p, i)
        send_own(p, zo)
    pass_near(0, zo)
    pass_near(1, zo)

    def gate_up(h):
        def body(j, carry):
            m = ((zh + h) % 2) * NX + (xi + j) % NX
            at = pl.ds(mo(m * 256, 256), 256)
            product = jnp.dot(rows[:, at], w_in[at, :], preferred_element_type=F32)
            acc[...] = acc[...] + product
            return carry

        lax.fori_loop(0, NX, body, 0)

    acc[...] = jnp.zeros_like(acc)
    wait_all(y1_wait, 0)
    wait_sibling(0, zh)
    wait_sibling(1, zh)
    gate_up(0)
    i = dp_of(zo, xi, core)
    wait_piece(2, i)
    send_own(2, zo)
    pass_far(0, zo)
    pass_far(1, zo)
    pass_near(2, zo)
    wait_all(y1_wait, 1)
    wait_sibling(0, zo)
    wait_sibling(1, zo)
    gate_up(1)
    gate = acc[:, 0:512]
    small = jnp.exp(-jnp.abs(gate))
    gated = gate * jnp.where(gate >= 0, 1.0, small) / (1.0 + small)
    hidden[...] = (gated * acc[:, 512:1024]).astype(BF)

    def down(j):
        i = chunk_slot(j)
        weights = jnp.concatenate([w_down[i + q] for q in range(4)], axis=1)
        partial[:, chunk_cols(j)] = jnp.dot(
            hidden[...], weights, preferred_element_type=F32
        ).astype(BF)
        start_all(y2_copy, j)
        from_y[own_y, chunk_cols(j)] = partial[own_y, chunk_cols(j)]

    def combine(j):
        wait_all(y2_wait, j)
        both = []
        for k in range(NK):
            left = from_y[2 * k * YBLK:(2 * k + 1) * YBLK, chunk_cols(j)].astype(F32)
            right = from_y[(2 * k + 1) * YBLK:(2 * k + 2) * YBLK, chunk_cols(j)].astype(F32)
            both.append((left + right).astype(BF))
        both = jnp.concatenate(both, axis=0)
        to_z[:, chunk_cols(j)] = jnp.dot(to_lines, both, preferred_element_type=F32).astype(BF)
        start_all(z2_copy, j)
        from_z[own_z, chunk_cols(j)] = to_z[own_z, chunk_cols(j)]

    def finish(j):
        wait_all(z2_wait, j)
        combined = from_z[:, chunk_cols(j)]
        total = jnp.dot(mix[0], combined, preferred_element_type=F32)
        total += jnp.dot(mix[1], combined, preferred_element_type=F32)
        total += jnp.dot(mix[2], combined, preferred_element_type=F32)
        out_ref[:, chunk_cols(j)] = total.astype(BF)

    wait_sibling(2, zh)
    down(0)
    down(1)
    pass_far(2, zo)
    combine(0)
    wait_sibling(2, zo)
    down(2)
    down(3)
    combine(1)
    combine(2)
    finish(0)
    combine(3)
    finish(1)
    finish(2)
    finish(3)

    for copy in sends:
        copy.wait_send()
    for h in (0, 1):
        sent_all(z1_copy, h)
        sent_all(y1_copy, h)
    for j in range(4):
        sent_all(y2_copy, j)
        sent_all(z2_copy, j)


def per_device(tokens, expert_ids, gate_values, capacity, w_in, w_down):
    dma = pltpu.SemaphoreType.DMA
    vmem = pl.BlockSpec(memory_space=pltpu.VMEM)
    hbm = pl.BlockSpec(memory_space=pl.ANY)
    call = pl.pallas_call(
        layer_kernel,
        out_shape=jax.ShapeDtypeStruct(tokens.shape, BF),
        in_specs=[hbm, vmem, vmem, vmem, hbm, hbm],
        out_specs=vmem,
        scratch_shapes=[
            pltpu.VMEM((128, 2048), BF),
            pltpu.VMEM((128, 2048), BF),
            pltpu.VMEM((128, 2048), BF),
            pltpu.VMEM((128, 2048), BF),
            pltpu.VMEM((256, 2048), BF),
            pltpu.VMEM((2048, 1024), BF),
            pltpu.VMEM((16, 512, 128), BF),
            pltpu.VMEM((128, 1024), BF),
            pltpu.VMEM((512, 128), BF),
            pltpu.VMEM((256, 1024), F32),
            pltpu.VMEM((256, 512), BF),
            pltpu.VMEM((256, 2048), BF),
            pltpu.VMEM((256, 2048), BF),
            pltpu.VMEM((128, 2048), BF),
            pltpu.VMEM((128, 2048), BF),
            pltpu.VMEM((3, 128, 128), BF),
            dma((3,)),
            dma((2, 8)), dma((2, 8)), dma((2, 8)), dma((2, 8)),
            dma((3, 16)), dma((3, 16)), dma((3,)),
            dma((4, 8)), dma((4, 8)), dma((4, 8)), dma((4, 8)),
        ],
        compiler_params=pltpu.CompilerParams(
            collective_id=0, has_side_effects=True, vmem_limit_bytes=40 * 1024 * 1024
        ),
        name="expert_layer",
    )
    return call(
        tokens,
        expert_ids.T,
        gate_values.T,
        capacity.reshape(1, -1),
        w_in[0],
        w_down[0],
    )


def solution(mesh):
    return jax.shard_map(
        per_device,
        mesh=mesh,
        in_specs=(
            P(("dp", "expert"), None),
            P(("dp", "expert"), None),
            P(("dp", "expert"), None),
            P(),
            P("expert", "dp", None),
            P("expert", None, "dp"),
        ),
        out_specs=P(("dp", "expert"), None),
        check_vma=False,
    )
```
